256 devices in a mesh: ctx: 16 (over z_lo, y, core), pb: 16 (over x, z_hi).
Axes of the slice: x: 4, y: 4, z: 8 (z_hi: 4, z_lo: 2; z = z_hi * 2 + z_lo), core: 2. Of those that a mesh axis runs over, the one named last changes fastest.
Arguments:
- queries: bfloat16 [256, 64, 8, 128], P('pb'), may hold values from -6 to 6
- keys: bfloat16 [16384, 128], P('ctx'), may hold values from -6 to 6
- values: bfloat16 [16384, 128], P('ctx'), may hold values from -6 to 6
- outputs_saved: bfloat16 [256, 64, 8, 128], P('pb'), may hold values from -6 to 6
- grad_out: bfloat16 [256, 64, 8, 128], P('pb'), may hold values from -6 to 6
- saved_lse: float32 [256, 64, 8], P('pb'), may hold values from 7 to 9
- block_lists: int32 [256, 96], P('pb'), may hold values from -1 to 127, as said below
Outputs:
- query_grad: float32 [256, 64, 8, 128], P('pb', 'ctx')
- key_grad: float32 [16384, 128], P(('ctx', 'pb'))
- value_grad: float32 [16384, 128], P(('ctx', 'pb'))
The draws below stay inside these ranges and needn't reach their ends.
Inputs may be any that keep to these rules, and one draw needn't show every extreme that they name: `block_lists`: each row lists distinct blocks in rising order, then -1 in the remaining entries. Of one row's blocks at most 6 lie in one run of 8 blocks (j * 8 to j * 8 + 7), and in every row exactly 6 lie in some such run.
All inputs are finite; a program needn't handle non-finite values.
Results may differ from the reference program's by a relative error of at most 0.0029.
Values sent between devices are 32-bit elements; how exact they have to be, the bound alone decides.
A program may use at most 128 MiB of HBM per device.

```python
import jax
import jax.numpy as jnp
from jax import lax

D_HEAD = 128
HEADS = 8
QLEN = 64
BLK = 128
CAP = 6
BLK_DEV = 8
QUESTIONS = 256
NB = 128
KEYS = 16384
LIST = 96


def draw_block_lists(key, part):
    shards = NB // BLK_DEV
    key_popular, key_count, key_hot, key_rank = jax.random.split(key, 4)
    popularity = jax.random.randint(key_popular, (1, shards), CAP // 2, CAP + 1)
    counts_shard = jax.random.randint(key_count, (QUESTIONS, shards), 0, popularity + 1)
    hot_shard = jax.random.randint(key_hot, (QUESTIONS, 1), 0, shards)
    counts_shard = jnp.where(jnp.arange(shards)[None, :] == hot_shard, CAP, counts_shard)
    raw_scores = jax.random.randint(key_rank, (QUESTIONS, shards, BLK_DEV), 0, 1 << 20)
    raw_scores = raw_scores * BLK_DEV + jnp.arange(BLK_DEV, dtype=jnp.int32)[None, None, :]
    rank_in = jnp.argsort(jnp.argsort(-raw_scores, axis=2, stable=True), axis=2, stable=True)
    member = (rank_in < counts_shard[:, :, None]).reshape(QUESTIONS, NB)
    block_ids = jnp.arange(NB, dtype=jnp.int32)[None, :]
    sort_score = jnp.where(member, 2 * NB - block_ids, NB - 1 - block_ids)
    top_values, top_index = jax.lax.top_k(sort_score, LIST)
    return jnp.where(top_values > NB, 2 * NB - top_values, -1).astype(jnp.int32)


def shard_levels(stream_key, dims, cuts, least, largest):
    factor_of = 1.0
    for position, parts in cuts:
        draws = jax.random.uniform(jax.random.fold_in(jax.random.fold_in(stream_key, 6), position), (parts,), jnp.float32, least / len(cuts), largest / len(cuts))
        factor_of = factor_of * jnp.repeat(jnp.exp(draws), dims[position] // parts).reshape((-1,) + (1,) * (len(dims) - 1 - position))
    return factor_of


def gaussian(rng, extent, spread, limit, pieces=(), kind=jnp.bfloat16):
    gain = shard_levels(rng, extent, pieces, -0.22, 0.18) if pieces else 1.0
    array = jax.random.normal(rng, extent, jnp.float32) * spread * gain
    return jnp.minimum(jnp.maximum(array, -limit), limit).astype(kind)


def setup_inputs(seed: int = 0) -> dict:
    splits = jax.random.split(jax.random.key(seed), 8)
    queries = gaussian(splits[0], (QUESTIONS, QLEN, HEADS, D_HEAD), 1.0, 6.0, ((0, 16),))
    keys = gaussian(splits[1], (KEYS, D_HEAD), 1.0, 6.0, ((0, 16),))
    values = gaussian(splits[2], (KEYS, D_HEAD), 1.0, 6.0, ((0, 16),))
    outputs_saved = gaussian(splits[3], (QUESTIONS, QLEN, HEADS, D_HEAD), 1.0, 6.0, ((0, 16),))
    grad_out = gaussian(splits[4], (QUESTIONS, QLEN, HEADS, D_HEAD), 1.0, 6.0, ((0, 16),))
    saved_lse = jnp.clip(7.0 + 2.0 * jax.random.uniform(splits[5], (QUESTIONS, QLEN, HEADS), jnp.float32) ** shard_levels(splits[5], (QUESTIONS, QLEN, HEADS), ((0, 16),), -0.2, 0.2), 7.0, 9.0)
    block_lists = draw_block_lists(jax.random.fold_in(splits[7], 71), 0)
    return {"queries": queries, "keys": keys, "values": values, "outputs_saved": outputs_saved, "grad_out": grad_out, "saved_lse": saved_lse, "block_lists": block_lists}


def reference(queries, keys, values, outputs_saved, grad_out, saved_lse, block_lists):
    factor = D_HEAD ** -0.5
    key_blocks = keys.reshape(NB, BLK, D_HEAD)
    value_blocks = values.reshape(NB, BLK, D_HEAD)
    row_delta = jnp.sum(grad_out.astype(jnp.float32) * outputs_saved.astype(jnp.float32), axis=-1)

    def question_step(totals, element):
        key_acc, value_acc = totals
        q_all, dout_all, lse_all, delta_all, listing = element
        live_slots = listing >= 0
        chosen = jnp.where(live_slots, listing, 0).astype(jnp.int32)
        key_slab = key_blocks[chosen].reshape(LIST * BLK, D_HEAD).astype(jnp.float32)
        value_slab = value_blocks[chosen].reshape(LIST * BLK, D_HEAD).astype(jnp.float32)
        live_cols = jnp.repeat(live_slots, BLK)
        q_rows = q_all.reshape(QLEN * HEADS, D_HEAD).astype(jnp.float32)
        dout_rows = dout_all.reshape(QLEN * HEADS, D_HEAD).astype(jnp.float32)
        scores = factor * jnp.dot(q_rows, key_slab.T, preferred_element_type=jnp.float32)
        prob_tile = jnp.where(live_cols[None, :], jnp.exp(scores - lse_all.reshape(-1)[:, None]), 0.0)
        dprob_tile = jnp.dot(dout_rows, value_slab.T, preferred_element_type=jnp.float32)
        dscore = (prob_tile * (dprob_tile - delta_all.reshape(-1)[:, None])).astype(jnp.bfloat16)
        prob_low = prob_tile.astype(jnp.bfloat16)
        dscore_wide = dscore.astype(jnp.float32)
        query_part = factor * jnp.dot(dscore_wide, key_slab, preferred_element_type=jnp.float32)
        key_part = factor * jnp.dot(dscore_wide.T, q_rows, preferred_element_type=jnp.float32)
        value_part = jnp.dot(prob_low.astype(jnp.float32).T, dout_rows, preferred_element_type=jnp.float32)
        weight_live = live_slots.astype(key_part.dtype)[:, None, None]
        key_acc = key_acc.at[chosen].add(key_part.reshape(LIST, BLK, D_HEAD) * weight_live)
        value_acc = value_acc.at[chosen].add(value_part.reshape(LIST, BLK, D_HEAD) * weight_live)
        return (key_acc, value_acc), query_part.reshape(QLEN, HEADS, D_HEAD)

    zero_acc = jnp.zeros((NB, BLK, D_HEAD), jnp.float32)
    (key_acc, value_acc), query_grad = lax.scan(
        question_step, (zero_acc, zero_acc), (queries, grad_out, saved_lse, row_delta, block_lists))
    return query_grad, key_acc.reshape(KEYS, D_HEAD), value_acc.reshape(KEYS, D_HEAD)
```

```python
from functools import partial

import jax
import jax.numpy as jnp
from jax import lax
from jax.experimental import pallas as pl
from jax.experimental.pallas import tpu as pltpu
from jax.sharding import PartitionSpec as P

BLK = 128
CAP = 6
BLK_DEV = 8
D = 128
MESH = pl.DeviceIdType.MESH

NT = (((1,), (1,)), ((), ()))
NN = (((1,), (0,)), ((), ()))


def dot(a, b, dims):
    return lax.dot_general(a, b, dims, preferred_element_type=jnp.float32)


def tiles_kernel(per_step, rows, lists_ref, q_ref, do_ref, o_ref, lse_ref, k_ref, v_ref,
                 qg_ref, kv_ref, kt_ref, delta_ref, acc_ref):
    factor = D ** -0.5
    step = pl.program_id(0)
    first = lax.axis_index("ctx") * BLK_DEV
    width = lists_ref.shape[1]
    dests = qg_ref.shape[0]
    part = rows // dests

    @pl.when(step == 0)
    def _():
        kv_ref[...] = jnp.zeros_like(kv_ref)
        for b in range(BLK_DEV):
            kt_ref[b] = k_ref[pl.ds(b * BLK, BLK), :].T

    ones = jnp.ones((8, 2 * D), jnp.bfloat16)

    def question(local, _):
        row = step * per_step + local
        prod = do_ref[local].astype(jnp.float32) * o_ref[local].astype(jnp.float32)
        high = prod.astype(jnp.bfloat16)
        low = (prod - high.astype(jnp.float32)).astype(jnp.bfloat16)
        delta_ref[...] = dot(ones, jnp.concatenate([high, low], axis=1), NT)
        acc_ref[...] = jnp.zeros_like(acc_ref)

        def probe(_, span):
            low_end, high_end = span
            mid = (low_end + high_end) // 2
            entry = lists_ref[row, jnp.minimum(mid, width - 1)]
            less = (entry >= 0) & (entry < first) & (mid < high_end)
            return jnp.where(less, mid + 1, low_end), jnp.where(less, high_end, mid)

        start, _ = lax.fori_loop(0, 7, probe, (jnp.int32(0), jnp.int32(width)), unroll=True)
        block_of = []
        count = jnp.int32(0)
        for j in range(CAP):
            at = start + j
            entry = lists_ref[row, jnp.minimum(at, width - 1)] - first
            inside = (at < width) & (entry >= 0) & (entry < BLK_DEV)
            count = count + inside.astype(jnp.int32)
            block_of.append(jnp.clip(entry, 0, BLK_DEV - 1))

        def tile(blocks):
            q = q_ref[local]
            do = do_ref[local]
            kb = jnp.concatenate([k_ref[pl.ds(pl.multiple_of(b * BLK, BLK), BLK), :] for b in blocks], axis=0)
            vb = jnp.concatenate([v_ref[pl.ds(pl.multiple_of(b * BLK, BLK), BLK), :] for b in blocks], axis=0)
            kt = jnp.concatenate([kt_ref[b] for b in blocks], axis=1)
            prob = jnp.exp(dot(kb, q, NT) * factor - lse_ref[local])
            dprob = dot(vb, do, NT)
            dscore = (prob * (dprob - delta_ref[0:1, :])).astype(jnp.bfloat16)
            value_part = dot(prob.astype(jnp.bfloat16), do, NN)
            key_part = dot(dscore, q, NN) * factor
            acc_ref[...] += dot(kt, dscore, NN)
            for j, b in enumerate(blocks):
                for h in range(2):
                    piece = slice(j * BLK + h * (BLK // 2), j * BLK + (h + 1) * (BLK // 2))
                    kv_ref[2 * b + h, 0] += key_part[piece]
                    kv_ref[2 * b + h, 1] += value_part[piece]

        for j in range(0, CAP, 2):
            @pl.when(count >= j + 2)
            def _():
                tile([block_of[j], block_of[j + 1]])

            @pl.when(count == j + 1)
            def _():
                tile([block_of[j]])

        grad = acc_ref[...].T * factor
        for s in range(dests):
            z, y, c = s // 8, (s // 2) % 4, s % 2
            qg_ref[c * 8 + z * 4 + y, local] = grad[s * part:(s + 1) * part]
        return 0

    lax.fori_loop(0, per_step, question, 0)


def tiles(queries, keys, values, outputs_saved, grad_out, saved_lse, block_lists, dests, groups, per_step):
    questions, qlen, heads, width = queries.shape
    rows = qlen * heads
    part = rows // dests
    flat = lambda a: a.reshape(questions, rows, width)
    block = pl.BlockSpec((per_step, rows, width), lambda i: (i, 0, 0))
    whole = pl.BlockSpec(keys.shape, lambda i: (0, 0))
    return pl.pallas_call(
        partial(tiles_kernel, per_step, rows),
        grid=(questions // per_step,),
        in_specs=[
            pl.BlockSpec(memory_space=pltpu.SMEM),
            block, block, block,
            pl.BlockSpec((per_step, 1, rows), lambda i: (i, 0, 0)),
            whole, whole,
        ],
        out_specs=[
            pl.BlockSpec((dests, per_step, part, width), lambda i: (0, i, 0, 0)),
            pl.BlockSpec((groups, 2, keys.shape[0] // groups, width), lambda i: (0, 0, 0, 0)),
        ],
        out_shape=[
            jax.ShapeDtypeStruct((dests, questions, part, width), jnp.float32),
            jax.ShapeDtypeStruct((groups, 2, keys.shape[0] // groups, width), jnp.float32),
        ],
        scratch_shapes=[
            pltpu.VMEM((BLK_DEV, width, BLK), jnp.bfloat16),
            pltpu.VMEM((8, rows), jnp.float32),
            pltpu.VMEM((width, rows), jnp.float32),
        ],
        compiler_params=pltpu.CompilerParams(dimension_semantics=("arbitrary",)),
        name="tiles",
    )(block_lists, flat(queries), flat(grad_out), flat(outputs_saved),
      saved_lse.reshape(questions, 1, rows), keys, values)


def reduce_kernel(pieces, qp_ref, kv_ref, qout_ref, kout_ref, vout_ref,
                  acc, other, relay_l, relay_r, from_l, from_r, from_z,
                  kacc, krelay_l, krelay_r, kfrom_l, kfrom_r, kfrom_z,
                  load_sem, send_sem, recv_sem, ksend_sem, krecv_sem):
    ctx, pb = lax.axis_index("ctx"), lax.axis_index("pb")
    c, y, z = ctx % 2, (ctx // 2) % 4, ctx // 8
    x, w = pb // 4, pb % 4
    yn, yp, yo = (y + 1) % 4, (y + 3) % 4, (y + 2) % 4
    xn, xp, xo = (x + 1) % 4, (x + 3) % 4, (x + 2) % 4
    at_ctx = lambda z_, y_, c_: {"ctx": z_ * 8 + y_ * 2 + c_}
    at_pb = lambda x_, w_: {"pb": x_ * 4 + w_}
    mate, right, left, across = at_ctx(z, y, 1 - c), at_ctx(z, yn, c), at_ctx(z, yp, c), at_ctx(1 - z, y, c)
    kright, kleft = at_pb(xn, w), at_pb(xp, w)
    kfar = [at_pb(x, (w + d) % 4) for d in (1, 2, 3)]
    n = qp_ref.shape[3] // pieces
    h = n // 2

    loads = [
        pltpu.make_async_copy(qp_ref.at[c, :, :, pl.ds(p * n, n)], acc.at[:, :, pl.ds(p * n, n)], load_sem.at[p])
        for p in range(pieces)
    ]
    kload = pltpu.make_async_copy(kv_ref, kacc, load_sem.at[pieces])
    for copy in loads + [kload]:
        copy.start()

    barrier = pltpu.get_barrier_semaphore()
    partners = [mate, right, left, across, kright, kleft] + kfar
    for device in partners:
        pl.semaphore_signal(barrier, inc=1, device_id=device, device_id_type=MESH)
    pl.semaphore_wait(barrier, len(partners))

    def remote(src, dst, sems, at, device):
        return pltpu.make_async_remote_copy(
            src_ref=src, dst_ref=dst, send_sem=sems[0].at[at], recv_sem=sems[1].at[at],
            device_id=device, device_id_type=MESH)

    qsems, ksems = (send_sem, recv_sem), (ksend_sem, krecv_sem)
    copies = {}
    for p in range(pieces):
        every, one, two = pl.ds(p * n, n), pl.ds(p * n, h), pl.ds(p * n + h, h)
        make = lambda k, src, dst, device: remote(src, dst, qsems, p * 8 + k, device)
        copies[p] = [
            make(0, qp_ref.at[1 - c, :, :, every], other.at[:, :, every], mate),
            make(1, acc.at[:, yo, one], relay_l.at[p], right),
            make(2, acc.at[:, yo, two], relay_r.at[p], left),
            make(3, acc.at[:, yn, two], from_l.at[p, 1], right),
            make(4, acc.at[:, yp, one], from_r.at[p, 0], left),
            make(5, acc.at[:, yn, one], from_l.at[p, 0], right),
            make(6, acc.at[:, yp, two], from_r.at[p, 1], left),
            make(7, acc.at[1 - z, y, every], from_z.at[p], across),
        ]
    one, two = pl.ds(0, 2), pl.ds(2, 2)
    make = lambda k, src, dst, device: remote(src, dst, ksems, k, device)
    kcopies = [
        make(0, kv_ref.at[xo, one], krelay_l, kright),
        make(1, kv_ref.at[xo, two], krelay_r, kleft),
        make(2, kv_ref.at[xn, two], kfrom_l.at[1], kright),
        make(3, kv_ref.at[xp, one], kfrom_r.at[0], kleft),
        make(4, kacc.at[xn, one], kfrom_l.at[0], kright),
        make(5, kacc.at[xp, two], kfrom_r.at[1], kleft),
    ] + [make(6 + i, kacc.at[x, (w + i + 1) % 4], kfrom_z.at[i], kfar[i]) for i in range(3)]

    for p in range(pieces):
        copies[p][0].start()
        if p == 0:
            for copy in kcopies[:4]:
                copy.start()

    def mated(p):
        every = pl.ds(p * n, n)
        loads[p].wait()
        copies[p][0].wait_recv()
        acc[:, :, every] += other[:, :, every]
        for copy in copies[p][1:5]:
            copy.start()

    def relayed(p):
        one, two = pl.ds(p * n, h), pl.ds(p * n + h, h)
        copies[p][1].wait_recv()
        acc[:, yn, one] += relay_l[p]
        copies[p][5].start()
        copies[p][2].wait_recv()
        acc[:, yp, two] += relay_r[p]
        copies[p][6].start()

    def joined(p):
        for copy in copies[p][3:7]:
            copy.wait_recv()
        for i in range(2):
            part = pl.ds(p * n + i * h, h)
            acc[:, y, part] += from_l[p, i] + from_r[p, i]
        copies[p][7].start()

    def finished(p):
        every = pl.ds(p * n, n)
        copies[p][7].wait_recv()
        qout_ref[every] = acc[z, y, every] + from_z[p]

    def krelayed():
        kload.wait()
        kcopies[0].wait_recv()
        kacc[xn, one] += krelay_l[...]
        kcopies[4].start()
        kcopies[1].wait_recv()
        kacc[xp, two] += krelay_r[...]
        kcopies[5].start()

    def kjoined():
        for copy in kcopies[2:6]:
            copy.wait_recv()
        for i in range(2):
            kacc[x, pl.ds(2 * i, 2)] += kfrom_l[i] + kfrom_r[i]
        for copy in kcopies[6:]:
            copy.start()

    def kfinished():
        for copy in kcopies[6:]:
            copy.wait_recv()
        total = kacc[x, w] + kfrom_z[0] + kfrom_z[1] + kfrom_z[2]
        kout_ref[...] = total[0]
        vout_ref[...] = total[1]

    for t in range(pieces + 3):
        if t < pieces:
            mated(t)
        if t == 1:
            krelayed()
        if 0 <= t - 1 < pieces:
            relayed(t - 1)
        if t == pieces - 1:
            kjoined()
        if 0 <= t - 2 < pieces:
            joined(t - 2)
        if t == pieces + 1:
            kfinished()
        if 0 <= t - 3 < pieces:
            finished(t - 3)
    for p in range(pieces):
        for copy in copies[p]:
            copy.wait_send()
    for copy in kcopies:
        copy.wait_send()


def reduce(qp, kv, pieces):
    _, _, _, questions, part, width = qp.shape
    n = questions // pieces
    h = n // 2
    keys = kv.shape[3]
    f32 = jnp.float32
    anywhere, vmem = pl.BlockSpec(memory_space=pl.ANY), pl.BlockSpec(memory_space=pltpu.VMEM)
    return pl.pallas_call(
        partial(reduce_kernel, pieces),
        in_specs=[anywhere, anywhere],
        out_specs=[vmem] * 3,
        out_shape=[
            jax.ShapeDtypeStruct((questions, part, width), f32),
            jax.ShapeDtypeStruct((keys, width), f32),
            jax.ShapeDtypeStruct((keys, width), f32),
        ],
        scratch_shapes=[
            pltpu.VMEM((2, 4, questions, part, width), f32),
            pltpu.VMEM((2, 4, questions, part, width), f32),
            pltpu.VMEM((pieces, 2, h, part, width), f32),
            pltpu.VMEM((pieces, 2, h, part, width), f32),
            pltpu.VMEM((pieces, 2, 2, h, part, width), f32),
            pltpu.VMEM((pieces, 2, 2, h, part, width), f32),
            pltpu.VMEM((pieces, n, part, width), f32),
            pltpu.VMEM((4, 4, 2, keys, width), f32),
            pltpu.VMEM((2, 2, keys, width), f32),
            pltpu.VMEM((2, 2, keys, width), f32),
            pltpu.VMEM((2, 2, 2, keys, width), f32),
            pltpu.VMEM((2, 2, 2, keys, width), f32),
            pltpu.VMEM((3, 2, keys, width), f32),
            pltpu.SemaphoreType.DMA((pieces + 1,)),
            pltpu.SemaphoreType.DMA((pieces * 8,)),
            pltpu.SemaphoreType.DMA((pieces * 8,)),
            pltpu.SemaphoreType.DMA((9,)),
            pltpu.SemaphoreType.DMA((9,)),
        ],
        compiler_params=pltpu.CompilerParams(collective_id=0, has_side_effects=True),
        name="reduce",
    )(qp, kv)


PER_STEP = 4
PIECES = 4


def local(queries, keys, values, outputs_saved, grad_out, saved_lse, block_lists):
    questions, qlen, heads, width = queries.shape
    qg, kv = tiles(queries, keys, values, outputs_saved, grad_out, saved_lse, block_lists, 16, 16, PER_STEP)
    qg = qg.reshape(2, 2, 4, questions, qg.shape[2], width)
    kv = kv.reshape(4, 4, 2, kv.shape[2], width)
    query_grad, key_grad, value_grad = reduce(qg, kv, PIECES)
    return (query_grad.reshape(questions, -1, heads, width), key_grad, value_grad)


def solution(mesh):
    placed = (
        P("pb", None, None, None),
        P("ctx", None),
        P("ctx", None),
        P("pb", None, None, None),
        P("pb", None, None, None),
        P("pb", None, None),
        P("pb", None),
    )
    return jax.shard_map(
        local,
        mesh=mesh,
        in_specs=placed,
        out_specs=(P("pb", "ctx", None, None), P(("ctx", "pb"), None), P(("ctx", "pb"), None)),
        check_vma=False,
    )
```

```python
from functools import partial

import jax
import jax.numpy as jnp
from jax import lax
from jax.experimental import pallas as pl
from jax.experimental.pallas import tpu as pltpu
from jax.sharding import PartitionSpec as P

BLK = 128
CAP = 6
BLK_DEV = 8
D = 128
PIECES = 8
GROUP = 2
MESH = pl.DeviceIdType.MESH
LOG2E = 1.4426950408889634

NT = (((1,), (1,)), ((), ()))
NN = (((1,), (0,)), ((), ()))


def dot(a, b, dims):
    return lax.dot_general(a, b, dims, preferred_element_type=jnp.float32)


def slot_table(lists, first):
    questions = lists.shape[0]
    lane = lax.broadcasted_iota(jnp.int32, (questions, 128), 1)
    table = jnp.where(lane < 8, BLK_DEV, CAP)
    count = jnp.zeros((questions, 1), jnp.int32)
    for b in range(BLK_DEV):
        member = jnp.max(jnp.where(lists == first + b, 1, 0), axis=1, keepdims=True)
        table = jnp.where((member > 0) & (lane == count), b, table)
        table = jnp.where((member > 0) & (lane == 8 + b), count, table)
        count = count + member
    return table


def lse_lines(lse):
    questions, heads, tokens = lse.shape
    rows = tokens * heads
    flat = lse.reshape(questions * heads, tokens)
    high = flat.astype(jnp.bfloat16)
    rest = flat - high.astype(jnp.float32)
    mid = rest.astype(jnp.bfloat16)
    low = (rest - mid.astype(jnp.float32)).astype(jnp.bfloat16)
    token = lax.broadcasted_iota(jnp.int32, (tokens, rows), 0)
    column = lax.broadcasted_iota(jnp.int32, (tokens, rows), 1)
    spread = jnp.where(token == column // heads, 1.0, 0.0).astype(jnp.bfloat16)
    wide = dot(high, spread, NN) + dot(mid, spread, NN) + dot(low, spread, NN)
    wide = wide.reshape(questions, heads, rows)
    head = lax.broadcasted_iota(jnp.int32, (questions, heads, rows), 1)
    column = lax.broadcasted_iota(jnp.int32, (questions, heads, rows), 2)
    return jnp.sum(jnp.where(head == column % heads, wide, 0.0), axis=1, keepdims=True)


def fused_kernel(lists_ref, lse_ref, q_hbm, do_hbm, o_hbm, k_hbm, v_hbm, qout_ref, kvout_ref,
                 q_buf, do_buf, o_buf, kx, vx, ktx, lines, table_v, table, slots, kv,
                 qp, other, relay_l, relay_r, from_l, from_r, from_z,
                 krelay_l, krelay_r, kfrom_l, kfrom_r, kfrom_z,
                 load_sem, base_sem, send_sem, recv_sem, ksend_sem, krecv_sem):
    factor = D ** -0.5
    ctx, pb = lax.axis_index("ctx"), lax.axis_index("pb")
    c, y, z = ctx % 2, (ctx // 2) % 4, ctx // 8
    x, w = pb // 4, pb % 4
    yn, yp, yo = (y + 1) % 4, (y + 3) % 4, (y + 2) % 4
    xn, xp, xo = (x + 1) % 4, (x + 3) % 4, (x + 2) % 4
    at_ctx = lambda z_, y_, c_: {"ctx": z_ * 8 + y_ * 2 + c_}
    at_pb = lambda x_, w_: {"pb": x_ * 4 + w_}
    mate, right, left, across = at_ctx(z, y, 1 - c), at_ctx(z, yn, c), at_ctx(z, yp, c), at_ctx(1 - z, y, c)
    kright, kleft = at_pb(xn, w), at_pb(xp, w)
    kfar = [at_pb(x, (w + d) % 4) for d in (1, 2, 3)]
    n = q_buf.shape[0] // PIECES
    h = n // 2
    part = qp.shape[4]

    def loads(p):
        every = pl.ds(p * n, n)
        return [
            pltpu.make_async_copy(src.at[every], dst.at[every], load_sem.at[p, i])
            for i, (src, dst) in enumerate(((q_hbm, q_buf), (do_hbm, do_buf), (o_hbm, o_buf)))
        ]

    base = [
        pltpu.make_async_copy(k_hbm, kx.at[pl.ds(0, BLK_DEV)], base_sem.at[0]),
        pltpu.make_async_copy(v_hbm, vx.at[pl.ds(0, BLK_DEV)], base_sem.at[1]),
    ]
    for copy in base:
        copy.start()
    for p in range(PIECES):
        for copy in loads(p):
            copy.start()

    barrier = pltpu.get_barrier_semaphore()
    partners = [mate, right, left, across, kright, kleft] + kfar
    for device in partners:
        pl.semaphore_signal(barrier, inc=1, device_id=device, device_id_type=MESH)

    table_v[...] = slot_table(lists_ref[...], ctx * BLK_DEV)
    move = pltpu.make_async_copy(table_v, table, base_sem.at[2])
    move.start()
    lines[...] = lse_lines(lse_ref[...]) * LOG2E
    kv[...] = jnp.zeros_like(kv)
    slots[...] = jnp.zeros_like(slots)
    for ref in (kx, vx, ktx):
        ref[BLK_DEV] = jnp.zeros_like(ref[BLK_DEV])
    for copy in base:
        copy.wait()
    for b in range(BLK_DEV):
        ktx[b] = kx[b].T
    move.wait()
    pl.semaphore_wait(barrier, len(partners))

    def remote(src, dst, send, recv, device):
        return pltpu.make_async_remote_copy(
            src_ref=src, dst_ref=dst, send_sem=send, recv_sem=recv,
            device_id=device, device_id_type=MESH)

    def copies(p):
        every, one, two = pl.ds(p * n, n), pl.ds(p * n, h), pl.ds(p * n + h, h)
        make = lambda k, src, dst, device: remote(src, dst, send_sem.at[p, k], recv_sem.at[p, k], device)
        return [
            make(0, qp.at[1 - c, :, :, every], other.at[:, :, every], mate),
            make(1, qp.at[c, :, yo, one], relay_l.at[p], right),
            make(2, qp.at[c, :, yo, two], relay_r.at[p], left),
            make(3, qp.at[c, :, yn, two], from_l.at[p, 1], right),
            make(4, qp.at[c, :, yp, one], from_r.at[p, 0], left),
            make(5, qp.at[c, :, yn, one], from_l.at[p, 0], right),
            make(6, qp.at[c, :, yp, two], from_r.at[p, 1], left),
            make(7, qp.at[c, 1 - z, y, every], from_z.at[p], across),
        ]

    def kcopies(g):
        one, two = pl.ds(0, 2), pl.ds(2, 2)
        make = lambda k, src, dst, device: remote(src, dst, ksend_sem.at[g, k], krecv_sem.at[g, k], device)
        return [
            make(0, kv.at[g, xo, one], krelay_l.at[g], kright),
            make(1, kv.at[g, xo, two], krelay_r.at[g], kleft),
            make(2, kv.at[g, xn, two], kfrom_l.at[g, 1], kright),
            make(3, kv.at[g, xp, one], kfrom_r.at[g, 0], kleft),
            make(4, kv.at[g, xn, one], kfrom_l.at[g, 0], kright),
            make(5, kv.at[g, xp, two], kfrom_r.at[g, 1], kleft),
        ] + [make(6 + i, kv.at[g, x, (w + i + 1) % 4], kfrom_z.at[g, i], kfar[i]) for i in range(3)]

    def mated(p):
        every = pl.ds(p * n, n)
        todo = copies(p)
        todo[0].wait_recv()
        qp[c, :, :, every] += other[:, :, every]
        for copy in todo[1:5]:
            copy.start()

    def relayed(p):
        one, two = pl.ds(p * n, h), pl.ds(p * n + h, h)
        todo = copies(p)
        todo[1].wait_recv()
        qp[c, :, yn, one] += relay_l[p]
        todo[5].start()
        todo[2].wait_recv()
        qp[c, :, yp, two] += relay_r[p]
        todo[6].start()

    def joined(p):
        todo = copies(p)
        for copy in todo[3:7]:
            copy.wait_recv()
        for i in range(2):
            half = pl.ds(p * n + i * h, h)
            qp[c, :, y, half] += from_l[p, i] + from_r[p, i]
        todo[7].start()

    def finished(p):
        every = pl.ds(p * n, n)
        copies(p)[7].wait_recv()
        qout_ref[every] = qp[c, z, y, every] + from_z[p]

    def kstart(g):
        for copy in kcopies(g)[:4]:
            copy.start()

    def krelayed(g):
        todo = kcopies(g)
        todo[0].wait_recv()
        kv[g, xn, pl.ds(0, 2)] += krelay_l[g]
        todo[4].start()
        todo[1].wait_recv()
        kv[g, xp, pl.ds(2, 2)] += krelay_r[g]
        todo[5].start()

    def kjoined(g):
        todo = kcopies(g)
        for copy in todo[2:6]:
            copy.wait_recv()
        for i in range(2):
            kv[g, x, pl.ds(2 * i, 2)] += kfrom_l[g, i] + kfrom_r[g, i]
        for copy in todo[6:]:
            copy.start()

    def kfinished(g):
        for copy in kcopies(g)[6:]:
            copy.wait_recv()
        kvout_ref[g] = kv[g, x, w] + kfrom_z[g, 0] + kfrom_z[g, 1] + kfrom_z[g, 2]

    ones = jnp.ones((8, 2 * D), jnp.bfloat16)

    def gather_slots(row, side):
        for b in range(BLK_DEV):
            slot = table[row, 8 + b]
            for g in range(2):
                at = (g, b // 2, pl.ds((2 * b) % 4, 2))
                kv[at] += slots[side, slot, g].reshape(2, BLK // 2, D)

    def question(row, side):
        gather_slots(jnp.maximum(row - 1, 0), 1 - side)
        q, do = q_buf[row], do_buf[row]
        prod = do.astype(jnp.float32) * o_buf[row].astype(jnp.float32)
        high = prod.astype(jnp.bfloat16)
        low = (prod - high.astype(jnp.float32)).astype(jnp.bfloat16)
        delta = dot(ones, jnp.concatenate([high, low], axis=1), NT)[0:1]
        line = lines[row]
        blocks = [table[row, s] for s in range(CAP)]
        dscores = []
        for j in range(0, CAP, GROUP):
            some = blocks[j:j + GROUP]
            kb = jnp.concatenate([kx[b] for b in some], axis=0)
            vb = jnp.concatenate([vx[b] for b in some], axis=0)
            prob = jnp.exp2(dot(kb, q, NT) * (factor * LOG2E) - line)
            dscore = (prob * (dot(vb, do, NT) - delta)).astype(jnp.bfloat16)
            value_part = dot(prob.astype(jnp.bfloat16), do, NN)
            key_part = dot(dscore, q, NN)
            dscores.append(dscore)
            for i in range(GROUP):
                slots[side, j + i, 0] = key_part[i * BLK:(i + 1) * BLK]
                slots[side, j + i, 1] = value_part[i * BLK:(i + 1) * BLK]
        kt = jnp.concatenate([ktx[b] for b in blocks], axis=1)
        grad = dot(kt, jnp.concatenate(dscores, axis=0), NN).T * factor
        for s in range(16):
            qp[s % 2, s // 8, (s // 2) % 4, row] = grad[s * part:(s + 1) * part]

    def piece(p, _):
        for copy in loads(p):
            copy.wait()
        for i in range(n):
            question(p * n + i, i % 2)
        copies(p)[0].start()
        for lag, stage in ((4, finished), (3, joined), (2, relayed), (1, mated)):
            @pl.when(p >= lag)
            def _():
                stage(p - lag)
        return 0

    lax.fori_loop(0, PIECES, piece, 0)
    last = PIECES - 1
    gather_slots(PIECES * n - 1, (n - 1) % 2)
    kstart(1)
    kv[0] = kv[0] * factor
    kstart(0)
    mated(last)
    relayed(last - 1)
    joined(last - 2)
    finished(last - 3)
    krelayed(1)
    relayed(last)
    krelayed(0)
    joined(last - 1)
    finished(last - 2)
    kjoined(1)
    joined(last)
    finished(last - 1)
    kjoined(0)
    finished(last)
    kfinished(1)
    kfinished(0)

    def sent(p, _):
        for copy in copies(p):
            copy.wait_send()
        return 0

    lax.fori_loop(0, PIECES, sent, 0)
    for g in range(2):
        for copy in kcopies(g):
            copy.wait_send()


def fused(queries, keys, values, outputs_saved, grad_out, saved_lse, block_lists):
    questions, qlen, heads, width = queries.shape
    rows = qlen * heads
    part = rows // 16
    n = questions // PIECES
    h = n // 2
    cut = keys.shape[0] // 16
    f32, bf16 = jnp.float32, jnp.bfloat16
    flat = lambda a: a.reshape(questions, rows, width)
    blocks = lambda a: a.reshape(BLK_DEV, BLK, width)
    anywhere, vmem = pl.BlockSpec(memory_space=pl.ANY), pl.BlockSpec(memory_space=pltpu.VMEM)
    return pl.pallas_call(
        fused_kernel,
        in_specs=[vmem, vmem] + [anywhere] * 5,
        out_specs=[vmem] * 2,
        out_shape=[
            jax.ShapeDtypeStruct((questions, part, width), f32),
            jax.ShapeDtypeStruct((2, cut, width), f32),
        ],
        scratch_shapes=[
            pltpu.VMEM((questions, rows, width), bf16),
            pltpu.VMEM((questions, rows, width), bf16),
            pltpu.VMEM((questions, rows, width), bf16),
            pltpu.VMEM((BLK_DEV + 1, BLK, width), bf16),
            pltpu.VMEM((BLK_DEV + 1, BLK, width), bf16),
            pltpu.VMEM((BLK_DEV + 1, width, BLK), bf16),
            pltpu.VMEM((questions, 1, rows), f32),
            pltpu.VMEM((questions, 128), jnp.int32),
            pltpu.SMEM((questions, 128), jnp.int32),
            pltpu.VMEM((2, CAP + 1, 2, BLK, width), f32),
            pltpu.VMEM((2, 4, 4, cut, width), f32),
            pltpu.VMEM((2, 2, 4, questions, part, width), f32),
            pltpu.VMEM((2, 4, questions, part, width), f32),
            pltpu.VMEM((PIECES, 2, h, part, width), f32),
            pltpu.VMEM((PIECES, 2, h, part, width), f32),
            pltpu.VMEM((PIECES, 2, 2, h, part, width), f32),
            pltpu.VMEM((PIECES, 2, 2, h, part, width), f32),
            pltpu.VMEM((PIECES, n, part, width), f32),
            pltpu.VMEM((2, 2, cut, width), f32),
            pltpu.VMEM((2, 2, cut, width), f32),
            pltpu.VMEM((2, 2, 2, cut, width), f32),
            pltpu.VMEM((2, 2, 2, cut, width), f32),
            pltpu.VMEM((2, 3, cut, width), f32),
            pltpu.SemaphoreType.DMA((PIECES, 3)),
            pltpu.SemaphoreType.DMA((3,)),
            pltpu.SemaphoreType.DMA((PIECES, 8)),
            pltpu.SemaphoreType.DMA((PIECES, 8)),
            pltpu.SemaphoreType.DMA((2, 9)),
            pltpu.SemaphoreType.DMA((2, 9)),
        ],
        compiler_params=pltpu.CompilerParams(collective_id=0, has_side_effects=True),
        name="fused",
    )(block_lists, saved_lse.transpose(0, 2, 1), flat(queries), flat(grad_out), flat(outputs_saved),
      blocks(keys), blocks(values))


def spread_kernel(q_ref, kv_ref, qout_ref, kout_ref, vout_ref):
    qout_ref[...] = q_ref[...]
    kout_ref[...] = kv_ref[0]
    vout_ref[...] = kv_ref[1]


def local(queries, keys, values, outputs_saved, grad_out, saved_lse, block_lists):
    questions, qlen, heads, width = queries.shape
    query_grad, both = fused(queries, keys, values, outputs_saved, grad_out, saved_lse, block_lists)
    vmem = pl.BlockSpec(memory_space=pltpu.VMEM)
    query_grad, key_grad, value_grad = pl.pallas_call(
        spread_kernel,
        in_specs=[vmem] * 2,
        out_specs=[vmem] * 3,
        out_shape=[jax.ShapeDtypeStruct(s, jnp.float32) for s in (query_grad.shape, both.shape[1:], both.shape[1:])],
        name="spread",
    )(query_grad, both)
    return (query_grad.reshape(questions, -1, heads, width), key_grad, value_grad)


def solution(mesh):
    placed = (
        P("pb", None, None, None),
        P("ctx", None),
        P("ctx", None),
        P("pb", None, None, None),
        P("pb", None, None, None),
        P("pb", None, None),
        P("pb", None),
    )
    return jax.shard_map(
        local,
        mesh=mesh,
        in_specs=placed,
        out_specs=(P("pb", "ctx", None, None), P(("ctx", "pb"), None), P(("ctx", "pb"), None)),
        check_vma=False,
    )
```

```python
from functools import partial

import jax
import jax.numpy as jnp
from jax import lax
from jax.experimental import pallas as pl
from jax.experimental.pallas import tpu as pltpu
from jax.sharding import PartitionSpec as P

BLK = 128
CAP = 6
BLK_DEV = 8
D = 128
PIECES = 8
MESH = pl.DeviceIdType.MESH
LOG2E = 1.4426950408889634

NT = (((1,), (1,)), ((), ()))
NN = (((1,), (0,)), ((), ()))


def dot(a, b, dims):
    return lax.dot_general(a, b, dims, preferred_element_type=jnp.float32)


def slot_table(lists, first):
    questions = lists.shape[0]
    lane = lax.broadcasted_iota(jnp.int32, (questions, 128), 1)
    table = jnp.where(lane < 8, BLK_DEV, CAP)
    count = jnp.zeros((questions, 1), jnp.int32)
    for b in range(BLK_DEV):
        member = jnp.max(jnp.where(lists == first + b, 1, 0), axis=1, keepdims=True)
        table = jnp.where((member > 0) & (lane == count), b, table)
        table = jnp.where((member > 0) & (lane == 8 + b), count, table)
        count = count + member
    return table


def lse_lines(lse):
    questions, heads, tokens = lse.shape
    rows = tokens * heads
    flat = lse.reshape(questions * heads, tokens)
    high = flat.astype(jnp.bfloat16)
    rest = flat - high.astype(jnp.float32)
    mid = rest.astype(jnp.bfloat16)
    low = (rest - mid.astype(jnp.float32)).astype(jnp.bfloat16)
    token = lax.broadcasted_iota(jnp.int32, (tokens, rows), 0)
    column = lax.broadcasted_iota(jnp.int32, (tokens, rows), 1)
    spread = jnp.where(token == column // heads, 1.0, 0.0).astype(jnp.bfloat16)
    wide = dot(high, spread, NN) + dot(mid, spread, NN) + dot(low, spread, NN)
    wide = wide.reshape(questions, heads, rows)
    head = lax.broadcasted_iota(jnp.int32, (questions, heads, rows), 1)
    column = lax.broadcasted_iota(jnp.int32, (questions, heads, rows), 2)
    return jnp.sum(jnp.where(head == column % heads, wide, 0.0), axis=1, keepdims=True)


def fused_kernel(lists_ref, lse_ref, q_hbm, do_hbm, o_hbm, k_hbm, v_hbm, qout_ref, kvout_ref,
                 q_buf, do_buf, o_buf, kx, vx, ktx, lines, table_v, table, slots, kvt, kv,
                 qp, other, relay_l, relay_r, from_l, from_r, from_z,
                 krelay_l, krelay_r, kfrom_l, kfrom_r, kfrom_z,
                 load_sem, base_sem, send_sem, recv_sem, ksend_sem, krecv_sem):
    factor = D ** -0.5
    ctx, pb = lax.axis_index("ctx"), lax.axis_index("pb")
    c, y, z = ctx % 2, (ctx // 2) % 4, ctx // 8
    x, w = pb // 4, pb % 4
    yn, yp, yo = (y + 1) % 4, (y + 3) % 4, (y + 2) % 4
    xn, xp, xo = (x + 1) % 4, (x + 3) % 4, (x + 2) % 4
    at_ctx = lambda z_, y_, c_: {"ctx": z_ * 8 + y_ * 2 + c_}
    at_pb = lambda x_, w_: {"pb": x_ * 4 + w_}
    mate, right, left, across = at_ctx(z, y, 1 - c), at_ctx(z, yn, c), at_ctx(z, yp, c), at_ctx(1 - z, y, c)
    kright, kleft = at_pb(xn, w), at_pb(xp, w)
    kfar = [at_pb(x, (w + d) % 4) for d in (1, 2, 3)]
    n = q_buf.shape[0] // PIECES
    h = n // 2
    part = qp.shape[4]

    def loads(p):
        every = pl.ds(p * n, n)
        return [
            pltpu.make_async_copy(src.at[every], dst.at[every], load_sem.at[p, i])
            for i, (src, dst) in enumerate(((q_hbm, q_buf), (do_hbm, do_buf), (o_hbm, o_buf)))
        ]

    base = [
        pltpu.make_async_copy(k_hbm, kx.at[pl.ds(0, BLK_DEV)], base_sem.at[0]),
        pltpu.make_async_copy(v_hbm, vx.at[pl.ds(0, BLK_DEV)], base_sem.at[1]),
    ]
    for copy in base:
        copy.start()
    for p in range(PIECES):
        for copy in loads(p):
            copy.start()

    barrier = pltpu.get_barrier_semaphore()
    partners = [mate, right, left, across, kright, kleft] + kfar
    for device in partners:
        pl.semaphore_signal(barrier, inc=1, device_id=device, device_id_type=MESH)

    table_v[...] = slot_table(lists_ref[...], ctx * BLK_DEV)
    move = pltpu.make_async_copy(table_v, table, base_sem.at[2])
    move.start()
    lines[...] = lse_lines(lse_ref[...]) * LOG2E
    kvt[...] = jnp.zeros_like(kvt)
    slots[...] = jnp.zeros_like(slots)
    for ref in (kx, vx, ktx):
        ref[BLK_DEV] = jnp.zeros_like(ref[BLK_DEV])
    for copy in base:
        copy.wait()
    for b in range(BLK_DEV):
        ktx[b] = kx[b].T
    move.wait()
    pl.semaphore_wait(barrier, len(partners))

    def remote(src, dst, send, recv, device):
        return pltpu.make_async_remote_copy(
            src_ref=src, dst_ref=dst, send_sem=send, recv_sem=recv,
            device_id=device, device_id_type=MESH)

    def copies(p):
        every, one, two = pl.ds(p * n, n), pl.ds(p * n, h), pl.ds(p * n + h, h)
        make = lambda k, src, dst, device: lambda: remote(src, dst, send_sem.at[p, k], recv_sem.at[p, k], device)
        return [
            make(0, qp.at[1 - c, :, :, every], other.at[:, :, every], mate),
            make(1, qp.at[c, :, yo, one], relay_l.at[p], right),
            make(2, qp.at[c, :, yo, two], relay_r.at[p], left),
            make(3, qp.at[c, :, yn, two], from_l.at[p, 1], right),
            make(4, qp.at[c, :, yp, one], from_r.at[p, 0], left),
            make(5, qp.at[c, :, yn, one], from_l.at[p, 0], right),
            make(6, qp.at[c, :, yp, two], from_r.at[p, 1], left),
            make(7, qp.at[c, 1 - z, y, every], from_z.at[p], across),
        ]

    def kcopies(g):
        one, two = pl.ds(0, 2), pl.ds(2, 2)
        make = lambda k, src, dst, device: lambda: remote(src, dst, ksend_sem.at[g, k], krecv_sem.at[g, k], device)
        return [
            make(0, kv.at[g, xo, one], krelay_l.at[g], kright),
            make(1, kv.at[g, xo, two], krelay_r.at[g], kleft),
            make(2, kv.at[g, xn, two], kfrom_l.at[g, 1], kright),
            make(3, kv.at[g, xp, one], kfrom_r.at[g, 0], kleft),
            make(4, kv.at[g, xn, one], kfrom_l.at[g, 0], kright),
            make(5, kv.at[g, xp, two], kfrom_r.at[g, 1], kleft),
        ] + [make(6 + i, kv.at[g, x, (w + i + 1) % 4], kfrom_z.at[g, i], kfar[i]) for i in range(3)]

    def mated(p):
        every = pl.ds(p * n, n)
        todo = copies(p)
        todo[0]().wait_recv()
        qp[c, :, :, every] += other[:, :, every]
        for copy in todo[1:5]:
            copy().start()

    def relayed(p):
        one, two = pl.ds(p * n, h), pl.ds(p * n + h, h)
        todo = copies(p)
        todo[1]().wait_recv()
        qp[c, :, yn, one] += relay_l[p]
        todo[5]().start()
        todo[2]().wait_recv()
        qp[c, :, yp, two] += relay_r[p]
        todo[6]().start()

    def joined(p):
        todo = copies(p)
        for copy in todo[3:7]:
            copy().wait_recv()
        for i in range(2):
            half = pl.ds(p * n + i * h, h)
            qp[c, :, y, half] += from_l[p, i] + from_r[p, i]
        todo[7]().start()

    def finished(p):
        every = pl.ds(p * n, n)
        copies(p)[7]().wait_recv()
        qout_ref[every] = qp[c, z, y, every] + from_z[p]

    def krelayed(g):
        todo = kcopies(g)
        todo[0]().wait_recv()
        kv[g, xn, pl.ds(0, 2)] += krelay_l[g]
        todo[4]().start()
        todo[1]().wait_recv()
        kv[g, xp, pl.ds(2, 2)] += krelay_r[g]
        todo[5]().start()

    def kjoined(g):
        todo = kcopies(g)
        for copy in todo[2:6]:
            copy().wait_recv()
        for i in range(2):
            kv[g, x, pl.ds(2 * i, 2)] += kfrom_l[g, i] + kfrom_r[g, i]
        for copy in todo[6:]:
            copy().start()

    def kfinished(g):
        for copy in kcopies(g)[6:]:
            copy().wait_recv()
        kvout_ref[g] = kv[g, x, w] + kfrom_z[g, 0] + kfrom_z[g, 1] + kfrom_z[g, 2]

    ones = jnp.ones((8, 2 * D), jnp.bfloat16)

    def gather_slots(rows):
        for b in range(BLK_DEV):
            at = [table[row, 8 + b] for row in rows]
            for g in range(2):
                kvt[g, b] += sum(slots[side, slot, g] for side, slot in enumerate(at))

    def flush(strip):
        for g in range(2):
            for i in range(2):
                block = kvt[g, 2 * strip + i].T
                block = block * factor if g == 0 else block
                kv[g, strip, pl.ds(2 * i, 2)] = block.reshape(2, BLK // 2, D)

    def scores_of(row):
        q, do = q_buf[row], do_buf[row]
        blocks = [table[row, s] for s in range(CAP)]
        prod = do.astype(jnp.float32) * o_buf[row].astype(jnp.float32)
        high = prod.astype(jnp.bfloat16)
        low = (prod - high.astype(jnp.float32)).astype(jnp.bfloat16)
        delta = dot(ones, jnp.concatenate([high, low], axis=1), NT)[0:1]
        kb = jnp.concatenate([kx[b] for b in blocks], axis=0)
        vb = jnp.concatenate([vx[b] for b in blocks], axis=0)
        prob = jnp.exp2(dot(kb, q, NT) * (factor * LOG2E) - lines[row])
        dscore = (prob * (dot(vb, do, NT) - delta)).astype(jnp.bfloat16)
        return prob.astype(jnp.bfloat16), dscore

    def sums_of(row, side, prob, dscore):
        value_part = dot(do_buf[row].T, prob, NT)
        key_part = dot(q_buf[row].T, dscore, NT)
        for s in range(CAP):
            slots[side, s, 0] = key_part[:, s * BLK:(s + 1) * BLK]
            slots[side, s, 1] = value_part[:, s * BLK:(s + 1) * BLK]
        kt = jnp.concatenate([ktx[table[row, s]] for s in range(CAP)], axis=1)
        grad = dot(kt, dscore, NN).T * factor
        for s in range(16):
            qp[s % 2, s // 8, (s // 2) % 4, row] = grad[s * part:(s + 1) * part]

    def piece(p, _):
        for copy in loads(p):
            copy.wait()
        gather_slots([jnp.maximum(p - 1, 0) * n + i for i in range(n)])
        for i in range(n):
            sums_of(p * n + i, i, *scores_of(p * n + i))
        copies(p)[0]().start()
        for lag, stage in ((4, finished), (3, joined), (2, relayed), (1, mated)):
            @pl.when(p >= lag)
            def _():
                stage(p - lag)
        return 0

    lax.fori_loop(0, PIECES, piece, 0)
    last = PIECES - 1
    gather_slots([last * n + i for i in range(n)])
    for strip, starts in ((xo, (0, 1)), (xn, (2,)), (xp, (3,)), (x, ())):
        flush(strip)
        for g in (1, 0):
            for k in starts:
                kcopies(g)[k]().start()
    mated(last)
    relayed(last - 1)
    joined(last - 2)
    finished(last - 3)
    krelayed(1)
    relayed(last)
    krelayed(0)
    joined(last - 1)
    finished(last - 2)
    kjoined(1)
    joined(last)
    finished(last - 1)
    kjoined(0)
    finished(last)
    kfinished(1)
    kfinished(0)

    def sent(p, _):
        for copy in copies(p):
            copy().wait_send()
        return 0

    lax.fori_loop(0, PIECES, sent, 0)
    for g in range(2):
        for copy in kcopies(g):
            copy().wait_send()


def fused(queries, keys, values, outputs_saved, grad_out, saved_lse, block_lists):
    questions, qlen, heads, width = queries.shape
    rows = qlen * heads
    part = rows // 16
    n = questions // PIECES
    h = n // 2
    cut = keys.shape[0] // 16
    f32, bf16 = jnp.float32, jnp.bfloat16
    flat = lambda a: a.reshape(questions, rows, width)
    blocks = lambda a: a.reshape(BLK_DEV, BLK, width)
    anywhere, vmem = pl.BlockSpec(memory_space=pl.ANY), pl.BlockSpec(memory_space=pltpu.VMEM)
    return pl.pallas_call(
        fused_kernel,
        in_specs=[vmem, vmem] + [anywhere] * 5,
        out_specs=[vmem] * 2,
        out_shape=[
            jax.ShapeDtypeStruct((questions, part, width), f32),
            jax.ShapeDtypeStruct((2, cut, width), f32),
        ],
        scratch_shapes=[
            pltpu.VMEM((questions, rows, width), bf16),
            pltpu.VMEM((questions, rows, width), bf16),
            pltpu.VMEM((questions, rows, width), bf16),
            pltpu.VMEM((BLK_DEV + 1, BLK, width), bf16),
            pltpu.VMEM((BLK_DEV + 1, BLK, width), bf16),
            pltpu.VMEM((BLK_DEV + 1, width, BLK), bf16),
            pltpu.VMEM((questions, 1, rows), f32),
            pltpu.VMEM((questions, 128), jnp.int32),
            pltpu.SMEM((questions, 128), jnp.int32),
            pltpu.VMEM((n, CAP + 1, 2, width, BLK), f32),
            pltpu.VMEM((2, BLK_DEV, width, BLK), f32),
            pltpu.VMEM((2, 4, 4, cut, width), f32),
            pltpu.VMEM((2, 2, 4, questions, part, width), f32),
            pltpu.VMEM((2, 4, questions, part, width), f32),
            pltpu.VMEM((PIECES, 2, h, part, width), f32),
            pltpu.VMEM((PIECES, 2, h, part, width), f32),
            pltpu.VMEM((PIECES, 2, 2, h, part, width), f32),
            pltpu.VMEM((PIECES, 2, 2, h, part, width), f32),
            pltpu.VMEM((PIECES, n, part, width), f32),
            pltpu.VMEM((2, 2, cut, width), f32),
            pltpu.VMEM((2, 2, cut, width), f32),
            pltpu.VMEM((2, 2, 2, cut, width), f32),
            pltpu.VMEM((2, 2, 2, cut, width), f32),
            pltpu.VMEM((2, 3, cut, width), f32),
            pltpu.SemaphoreType.DMA((PIECES, 3)),
            pltpu.SemaphoreType.DMA((3,)),
            pltpu.SemaphoreType.DMA((PIECES, 8)),
            pltpu.SemaphoreType.DMA((PIECES, 8)),
            pltpu.SemaphoreType.DMA((2, 9)),
            pltpu.SemaphoreType.DMA((2, 9)),
        ],
        compiler_params=pltpu.CompilerParams(collective_id=0, has_side_effects=True),
        name="fused",
    )(block_lists, saved_lse.transpose(0, 2, 1), flat(queries), flat(grad_out), flat(outputs_saved),
      blocks(keys), blocks(values))


def spread_kernel(q_ref, kv_ref, qout_ref, kout_ref, vout_ref):
    qout_ref[...] = q_ref[...]
    kout_ref[...] = kv_ref[0]
    vout_ref[...] = kv_ref[1]


def local(queries, keys, values, outputs_saved, grad_out, saved_lse, block_lists):
    questions, qlen, heads, width = queries.shape
    query_grad, both = fused(queries, keys, values, outputs_saved, grad_out, saved_lse, block_lists)
    vmem = pl.BlockSpec(memory_space=pltpu.VMEM)
    query_grad, key_grad, value_grad = pl.pallas_call(
        spread_kernel,
        in_specs=[vmem] * 2,
        out_specs=[vmem] * 3,
        out_shape=[jax.ShapeDtypeStruct(s, jnp.float32) for s in (query_grad.shape, both.shape[1:], both.shape[1:])],
        name="spread",
    )(query_grad, both)
    return (query_grad.reshape(questions, -1, heads, width), key_grad, value_grad)


def solution(mesh):
    placed = (
        P("pb", None, None, None),
        P("ctx", None),
        P("ctx", None),
        P("pb", None, None, None),
        P("pb", None, None, None),
        P("pb", None, None),
        P("pb", None),
    )
    return jax.shard_map(
        local,
        mesh=mesh,
        in_specs=placed,
        out_specs=(P("pb", "ctx", None, None), P(("ctx", "pb"), None), P(("ctx", "pb"), None)),
        check_vma=False,
    )
```
